256 devices in a mesh: blk: 16 (over x, z_hi), head: 16 (over y, z_lo, core).
Axes of the slice: x: 4, y: 4, z: 8 (z_hi: 4, z_lo: 2; z = z_hi * 2 + z_lo), core: 2. Of those that a mesh axis runs over, the one named last changes fastest.
Arguments:
- qkv_rows: bfloat16 [65536, 3, 1024], P(('blk', 'head')), may hold values from -10 to 10
- neighbours: int32 [512, 32], P('blk'), may hold values from 0 to 511, as said below
- w_out: bfloat16 [1024, 1024], replicated, may hold values from -0.1875 to 0.1875
Outputs:
- projected: bfloat16 [65536, 1024], P(('blk', 'head'))
The draws below stay inside these ranges and needn't reach their ends.
Inputs may be any that keep to these rules, and one draw needn't show every extreme that they name: `neighbours`: row b lists 32 different key blocks, the first being b itself; the others lie spread over the whole sequence.
All inputs are finite; a program needn't handle non-finite values.
Results may differ from the reference program's by a relative error of at most 0.0057.
Values may be sent and summed in bfloat16 or wider, within the bound.
No kernel may reach another device: no remote copies, remote signals or barrier semaphores. Data moves between devices by JAX's collectives and lax.ppermute only.
A program may use at most 128 MiB of HBM per device.

```python
import math
import jax
import jax.numpy as jnp
from jax import lax

HEADS = 16
HD = 64
D = 1024
BLOCK = 128
NBR = 32
TOKENS = 65536
NQB = 512


def neighbour_list(key):
    sub_key = jax.random.fold_in(key, 11)
    stride = NQB // NBR
    jitter = jax.random.randint(sub_key, (NQB, NBR), 0, stride)
    slot_ids = jnp.arange(NBR, dtype=jnp.int32)[None, :]
    offsets = jnp.where(slot_ids == 0, 0, slot_ids * stride + jitter)
    row_ids = jnp.arange(NQB, dtype=jnp.int32)[:, None]
    return ((row_ids + offsets) % NQB).astype(jnp.int32)


def draw_neighbours(key, part):
    return neighbour_list(key)


def draw_qkv_rows(key, part):
    base_key = jax.random.fold_in(key, 23)
    drawn = jnp.clip(jax.random.normal(base_key, (TOKENS, 3, D), jnp.float32), -6.0, 6.0)
    return drawn.astype(jnp.bfloat16)


def gaussian(rng, dims, width, reach, kind=jnp.bfloat16):
    array = jax.random.normal(rng, dims, jnp.float32) * width
    return jnp.minimum(jnp.maximum(array, -reach), reach).astype(kind)


def setup_inputs(seed: int = 0) -> dict:
    seeds = jax.random.split(jax.random.key(seed), 4)
    return {
        "qkv_rows": draw_qkv_rows(jax.random.fold_in(seeds[3], 71), 0),
        "neighbours": draw_neighbours(jax.random.fold_in(seeds[3], 71), 0),
        "w_out": gaussian(seeds[2], (D, D), D ** -0.5, 0.1875),
    }


def reference(qkv_rows, neighbours, w_out):
    scaling = 1.0 / math.sqrt(HD)
    queries = qkv_rows[:, 0].reshape(NQB, BLOCK, HEADS, HD)
    pairs = qkv_rows[:, 1:].reshape(NQB, BLOCK, 2, HEADS, HD)

    def attend_block(bundle):
        query_block, listed = bundle
        picked = pairs[listed]
        key_rows = picked[:, :, 0].reshape(NBR * BLOCK, HEADS, HD).astype(jnp.float32)
        value_rows = picked[:, :, 1].reshape(NBR * BLOCK, HEADS, HD).astype(jnp.float32)
        scores = jnp.einsum('qhd,khd->hqk', query_block.astype(jnp.float32), key_rows) * scaling
        scores = scores - lax.optimization_barrier(jnp.max(scores, axis=-1, keepdims=True))
        powers = jnp.exp(scores)
        weights = (powers / lax.optimization_barrier(jnp.sum(powers, axis=-1, keepdims=True))).astype(jnp.bfloat16)
        result_rows = jnp.einsum('hqk,khd->qhd', weights.astype(jnp.float32), value_rows)
        return result_rows.astype(jnp.bfloat16).reshape(BLOCK, HEADS * HD)
    attended = lax.map(attend_block, (queries, neighbours)).reshape(TOKENS, D)
    return jnp.dot(attended, w_out, preferred_element_type=jnp.float32).astype(jnp.bfloat16)
```

```python
import functools
import math

import jax
import jax.numpy as jnp
from jax import lax
from jax.experimental import pallas as pl
from jax.experimental.pallas import tpu as pltpu
from jax.sharding import Mesh
from jax.sharding import PartitionSpec as P

HD = 64
BLOCK = 128
NBR = 32
NULL = 128
LOW = -1e30
SCALE2 = math.log2(math.e) / math.sqrt(HD)
AXES = ("x", "zh", "y", "zl", "c")
ZC = ("zh", "zl", "c")
PIECES = (16, 16, 16, 8, 8)
BF = jnp.bfloat16
F32 = jnp.float32


def device_id(x, zh, y, zl, c):
    return ((((x % 4) * 4 + zh) * 4 + (y % 4)) * 2 + zl) * 2 + c


def shift(step, along_x):
    pairs = []
    for i in range(256):
        x, zh, y, zl, c = i // 64, i // 16 % 4, i // 4 % 4, i // 2 % 2, i % 2
        to = (x + step, y) if c == along_x else (x, y + step)
        pairs.append((i, device_id(to[0], zh, to[1], zl, c)))
    return pairs


def move_keys(v, step):
    return lax.ppermute(v, AXES, shift(step, 1))


def move_rows(v, step):
    return lax.ppermute(v, AXES, shift(step, 0))


def pack_kernel(x_ref, slab_ref, o_ref):
    q = x_ref[0]
    k = x_ref[1]
    vt = x_ref[2].T
    qt = q.T
    for h in range(2):
        lanes = slice(h * HD, (h + 1) * HD)
        o_ref[h, 0:128] = jnp.concatenate([k[:BLOCK, lanes], k[BLOCK:, lanes]], axis=1)
        for e in range(2):
            cols = slice(e * BLOCK, (e + 1) * BLOCK)
            o_ref[h, 128 + e * HD : 128 + (e + 1) * HD] = vt[lanes, cols]
            o_ref[h, 256 + e * HD : 256 + (e + 1) * HD] = qt[lanes, cols]
        o_ref[h, 384:400] = slab_ref[...]


def pack(qkv, slab):
    return pl.pallas_call(
        pack_kernel,
        grid=(8,),
        out_shape=jax.ShapeDtypeStruct((16, 400, 128), BF),
        in_specs=[
            pl.BlockSpec((3, 256, 128), lambda i: (0, 0, i)),
            pl.BlockSpec((16, 128), lambda i: (0, 0)),
        ],
        out_specs=pl.BlockSpec((2, 400, 128), lambda i: (i, 0, 0)),
        name="pack",
    )(jnp.transpose(qkv, (1, 0, 2)), slab)


def attend_kernel(streams, slots, kidx, vidx, cnt, *refs):
    pieces = sum(len(s) for s in slots)
    q_in, refs = refs[:pieces], refs[pieces:]
    kv_in, refs = refs[:5], refs[5:]
    outs, refs = refs[: len(slots)], refs[len(slots) :]
    kpk, k_scr, v_scr, q_scr, o_scr, l_scr, sem, osem, *s_bufs = refs
    nq = 32 * len(slots)
    kc, vc, qc = [], [], []
    at = 0
    for n, piece in zip(PIECES, kv_in):
        kc.append(pltpu.make_async_copy(piece.at[:, 0:2], kpk.at[pl.ds(at, n)], sem.at[len(kc)]))
        vc.append(
            pltpu.make_async_copy(piece.at[:, 2:4], v_scr.at[pl.ds(at, n), :, 0:HD], sem.at[5 + len(vc)])
        )
        at += n
    at = 0
    for n, piece in zip([n for s in slots for n in s], q_in):
        qc.append(
            pltpu.make_async_copy(piece.at[:, 0:128], q_scr.at[pl.ds(at, n)], sem.at[10 + len(qc)])
        )
        at += n
    for copy in kc + vc + qc:
        copy.start()
    v_scr[:, :, HD:, :] = jnp.ones((65, 2, 16, 128), BF)
    v_scr[64] = jnp.zeros((2, 80, 128), BF)
    low = lax.broadcasted_iota(jnp.int32, (128, 128), 1) < HD
    zero = jnp.zeros((128, 128), BF)
    for copy in kc:
        copy.wait()

    def split(i, carry):
        pair = kpk[i].reshape(128, 128)
        k_scr[2 * i] = jnp.where(low, pair, zero)
        k_scr[2 * i + 1] = jnp.where(low, zero, pair)
        return carry

    lax.fori_loop(0, 64, split, 0, unroll=4)
    for copy in vc + qc:
        copy.wait()
    per = nq // streams

    def total(s):
        return lax.fori_loop(s * per, (s + 1) * per, lambda q, t: t + cnt[q], jnp.int32(0))

    steps = total(0)
    for s in range(1, streams):
        steps = jnp.maximum(steps, total(s))

    def row(s, q):
        return jnp.minimum(q, (s + 1) * per - 1)

    def first(s, q, j):
        qr = row(s, q)
        base = qr * NBR + 2 * j
        qt = q_scr[lax.shift_right_logical(qr, 1), pl.ds(pl.multiple_of((qr & 1) * HD, HD), HD), :]
        keys = jnp.concatenate([k_scr[kidx[base]], k_scr[kidx[base + 1]]], axis=0)
        scores = jnp.dot(keys, jnp.concatenate([qt, qt], axis=0), preferred_element_type=F32)
        s_bufs[s][...] = scores
        return jnp.max(scores.reshape(32, 8, 128), axis=0)

    def second(s, q, j, top, m, acc):
        qr = row(s, q)
        base = qr * NBR + 2 * j
        va, vb = vidx[base], vidx[base + 1]
        m = jnp.where(j == 0, LOW, m)
        m_new = jnp.maximum(m, jnp.max(top, axis=0, keepdims=True))
        mc = m_new * SCALE2
        powers = jnp.exp2(s_bufs[s][...] * SCALE2 - mc).astype(BF)
        values = jnp.concatenate(
            [v_scr[lax.shift_right_logical(va, 1), va & 1], v_scr[lax.shift_right_logical(vb, 1), vb & 1]],
            axis=1,
        )
        acc = acc * jnp.exp2(m * SCALE2 - mc) + jnp.dot(values, powers, preferred_element_type=F32)
        l = acc[HD : HD + 1]
        lc = jnp.maximum(l, 1.0)
        to = jnp.where(q >= (s + 1) * per, nq, qr)
        o_scr[to] = (acc[:HD] * (1.0 / lc)).astype(BF)
        l_scr[pl.ds(to, 1), :] = jnp.where(l > 0, mc + jnp.log2(lc), LOW)
        last = j + 1 >= cnt[qr]
        return jnp.where(last, q + 1, q), jnp.where(last, 0, j + 1), m_new, acc

    def body(t, carry):
        state, top = list(carry[0]), carry[1]
        for s in range(streams):
            after = (s + 1) % streams
            next_top = first(after, state[after][0], state[after][1])
            q, j, m, acc = state[s]
            state[s] = second(s, q, j, top, m, acc)
            top = next_top
        return tuple(state), top

    start = tuple(
        (jnp.int32(s * per), jnp.int32(0), jnp.full((1, 128), LOW, F32), jnp.zeros((80, 128), F32))
        for s in range(streams)
    )
    lax.fori_loop(0, steps, body, (start, first(0, jnp.int32(0), jnp.int32(0))))
    copies = []
    for s in range(len(slots)):
        lse = l_scr[32 * s : 32 * (s + 1)]
        high = lse.astype(BF)
        rest = lse - high.astype(F32)
        mid = rest.astype(BF)
        tail = (rest - mid.astype(F32)).astype(BF)
        extra = o_scr.at[nq + 1 + 2 * s]
        extra[0:32] = high
        extra[32:64] = mid
        o_scr[nq + 2 + 2 * s] = jnp.concatenate([tail, tail], axis=0)
        copies.append(
            pltpu.make_async_copy(o_scr.at[pl.ds(32 * s, 32)], outs[s].at[pl.ds(0, 32)], osem.at[2 * s])
        )
        copies.append(
            pltpu.make_async_copy(
                o_scr.at[pl.ds(nq + 1 + 2 * s, 2)], outs[s].at[pl.ds(32, 2)], osem.at[2 * s + 1]
            )
        )
    for copy in copies:
        copy.start()
    for copy in copies:
        copy.wait()


def attend(lists, at, rows, kvs, streams):
    slots = [[p.shape[0] for p in s] for s in rows]
    flat = [p for s in rows for p in s]
    nq = 32 * len(slots)
    kidx, vidx, cnt = (v[at : at + nq].reshape(-1) for v in lists)
    anywhere = pl.BlockSpec(memory_space=pl.ANY)
    return pl.pallas_call(
        functools.partial(attend_kernel, streams, slots),
        out_shape=[jax.ShapeDtypeStruct((34, HD, 128), BF)] * len(slots),
        in_specs=[pl.BlockSpec(memory_space=pltpu.SMEM)] * 3 + [anywhere] * (len(flat) + 5),
        out_specs=[anywhere] * len(slots),
        scratch_shapes=[
            pltpu.VMEM((64, 2, 64, 128), BF),
            pltpu.VMEM((128, 128, 128), BF),
            pltpu.VMEM((65, 2, 80, 128), BF),
            pltpu.VMEM((nq // 2, 128, 128), BF),
            pltpu.VMEM((nq + 1 + 2 * len(slots), HD, 128), BF),
            pltpu.VMEM((nq + 8, 128), F32),
            pltpu.SemaphoreType.DMA((16,)),
            pltpu.SemaphoreType.DMA((8,)),
        ]
        + [pltpu.VMEM((256, 128), F32)] * streams,
        cost_estimate=pl.CostEstimate(
            flops=nq * 8 * 128 * 128 * 256, bytes_accessed=8 << 20, transcendentals=nq * 8 * 128 * 128
        ),
        name="attend",
    )(kidx, vidx, cnt, *flat, *kvs)


def merge_kernel(a_ref, b_ref, c_ref, d_ref, o_ref):
    refs = (a_ref, b_ref, c_ref, d_ref)
    lses = [
        r[32, 0:32].astype(F32) + r[32, 32:64].astype(F32) + r[33, 0:32].astype(F32) for r in refs
    ]
    top = functools.reduce(jnp.maximum, lses)
    weights = [jnp.exp2(l - top) for l in lses]
    scale = 1.0 / sum(weights)
    weights = [w * scale for w in weights]
    for q in range(32):
        o_ref[q] = sum(r[q].astype(F32) * w[q : q + 1] for r, w in zip(refs, weights)).astype(BF)


def merge(parts):
    return pl.pallas_call(
        merge_kernel,
        out_shape=jax.ShapeDtypeStruct((32, HD, 128), BF),
        name="merge",
    )(*parts)


def index_lists(slabs):
    v = slabs.astype(F32).reshape(64, 2, 2, NBR)
    ids = (v[:, :, 0] * 16 + v[:, :, 1]).astype(jnp.int32).reshape(128, NBR)
    core = lax.axis_index("c")
    xb, yb = ids // 128, ids // 8 % 4
    xm, ym = lax.axis_index("x"), lax.axis_index("y")
    valid = jnp.where(core == 0, xb == xm, yb == ym)
    ring = jnp.where(core == 0, yb - ym, xb - xm) & 3
    slot = jnp.where(ring == 0, 0, jnp.where(ring == 3, 1, ring + 1))
    local = slot * 32 + (ids // 32 % 4) * 8 + ids % 8
    before = jnp.arange(NBR)[:, None] < jnp.arange(NBR)[None, :]
    place = jnp.sum(jnp.where(before[None] & valid[:, :, None], 1, 0), axis=1)
    hit = valid[:, None, :] & (place[:, None, :] == jnp.arange(NBR)[None, :, None])
    found = jnp.sum(jnp.where(hit, local[:, None, :] + 1, 0), axis=2) - 1
    count = jnp.sum(valid.astype(jnp.int32), axis=1)
    vidx = jnp.where(found < 0, NULL, found)
    kidx = jnp.where(found < 0, jnp.maximum(found[:, :1], 0), found)
    return kidx, vidx, jnp.maximum((count + 1) // 2, 1)


def shards(qkv_rows, neighbours, w_out):
    mine = lax.axis_index("y") * 4 + lax.axis_index("zl") * 2 + lax.axis_index("c")
    own = lax.dynamic_slice(neighbours, (2 * mine, 0), (2, NBR))
    digits = jnp.stack([own // 16, own % 16], axis=1).reshape(1, 128).astype(BF)
    slab = jnp.broadcast_to(digits, (16, 128))
    chunks = lax.all_to_all(pack(qkv_rows, slab), ZC, split_axis=0, concat_axis=0, tiled=True)
    kv, rows = chunks[:, :256], chunks[:, 256:]
    kv_l, kv_r = move_keys(kv, 1), move_keys(kv, -1)
    q_l, q_r = move_rows(rows, 1), move_rows(rows, -1)
    kv_d0, kv_d1 = move_keys(kv_l[:8], 1), move_keys(kv_r[8:], -1)
    q_d0, q_d1 = move_rows(q_l[:8], 1), move_rows(q_r[8:], -1)
    lists = index_lists(jnp.concatenate([v[:, 128] for v in (rows, q_l, q_r, q_d0, q_d1)], axis=0))
    kvs = [v.reshape(-1, 4, 64, 128) for v in (kv, kv_l, kv_r, kv_d0, kv_d1)]
    far = attend(lists, 32, [[q_l], [q_r], [q_d0, q_d1]], kvs, 3)
    near = attend(lists, 0, [[rows]], kvs, 4)
    back = [move_rows(v, step) for v, step in zip(far, (-1, 1, 2))]
    attended = merge([near[0], *back]).reshape(16, 128, 128)
    arrived = lax.all_to_all(attended, ZC, split_axis=0, concat_axis=0, tiled=True)
    out = jnp.einsum(
        "hbdt,hdo->bto",
        arrived.reshape(16, 2, HD, 128),
        w_out.reshape(16, HD, 1024),
        preferred_element_type=F32,
    )
    return out.astype(BF).reshape(256, 1024)


def solution(mesh):
    grid = Mesh(mesh.devices.reshape(4, 4, 4, 2, 2), AXES)
    return jax.shard_map(
        shards,
        mesh=grid,
        in_specs=(P(AXES, None, None), P(("x", "zh"), None), P()),
        out_specs=P(AXES, None),
        check_vma=False,
    )
```

```python
import functools
import math

import jax
import jax.numpy as jnp
from jax import lax
from jax.experimental import pallas as pl
from jax.experimental.pallas import tpu as pltpu
from jax.sharding import Mesh
from jax.sharding import PartitionSpec as P

HD = 64
BLOCK = 128
NBR = 32
NULL = 128
LOW = -1e30
SCALE2 = math.log2(math.e) / math.sqrt(HD)
AXES = ("x", "zh", "y", "zl", "c")
ZC = ("zh", "zl", "c")
PIECES = (16, 16, 16, 8, 8)
BF = jnp.bfloat16
F32 = jnp.float32


def device_id(x, zh, y, zl, c):
    return ((((x % 4) * 4 + zh) * 4 + (y % 4)) * 2 + zl) * 2 + c


def shift(step, along_x):
    pairs = []
    for i in range(256):
        x, zh, y, zl, c = i // 64, i // 16 % 4, i // 4 % 4, i // 2 % 2, i % 2
        to = (x + step, y) if c == along_x else (x, y + step)
        pairs.append((i, device_id(to[0], zh, to[1], zl, c)))
    return pairs


def move_keys(v, step):
    return lax.ppermute(v, AXES, shift(step, 1))


def move_rows(v, step):
    return lax.ppermute(v, AXES, shift(step, 0))


def pack_kernel(x_ref, slab_ref, o_ref):
    q = x_ref[0]
    k = x_ref[1]
    vt = x_ref[2].T
    qt = q.T
    for h in range(2):
        lanes = slice(h * HD, (h + 1) * HD)
        o_ref[h, 0:128] = jnp.concatenate([k[:BLOCK, lanes], k[BLOCK:, lanes]], axis=1)
        for e in range(2):
            cols = slice(e * BLOCK, (e + 1) * BLOCK)
            o_ref[h, 128 + e * HD : 128 + (e + 1) * HD] = vt[lanes, cols]
            o_ref[h, 256 + e * HD : 256 + (e + 1) * HD] = qt[lanes, cols]
        o_ref[h, 384:400] = slab_ref[...]


def pack(qkv, slab):
    return pl.pallas_call(
        pack_kernel,
        grid=(8,),
        out_shape=jax.ShapeDtypeStruct((16, 400, 128), BF),
        in_specs=[
            pl.BlockSpec((3, 256, 128), lambda i: (0, 0, i)),
            pl.BlockSpec((16, 128), lambda i: (0, 0)),
        ],
        out_specs=pl.BlockSpec((2, 400, 128), lambda i: (i, 0, 0)),
        name="pack",
    )(jnp.transpose(qkv, (1, 0, 2)), slab)


def attend_kernel(streams, ahead, slots, kidx, vidx, cnt, *refs):
    pieces = sum(len(s) for s in slots)
    q_in, refs = refs[:pieces], refs[pieces:]
    kv_in, refs = refs[:5], refs[5:]
    outs, refs = refs[: len(slots)], refs[len(slots) :]
    kpk, k_scr, v_scr, q_scr, o_scr, l_scr, sem, osem, *s_bufs = refs
    nq = 32 * len(slots)
    kc, vc, qc = [], [], []
    at = 0
    for n, piece in zip(PIECES, kv_in):
        kc.append(pltpu.make_async_copy(piece.at[:, 0:2], kpk.at[pl.ds(at, n)], sem.at[len(kc)]))
        vc.append(
            pltpu.make_async_copy(piece.at[:, 2:4], v_scr.at[pl.ds(at, n), :, 0:HD], sem.at[5 + len(vc)])
        )
        at += n
    at = 0
    for n, piece in zip([n for s in slots for n in s], q_in):
        qc.append(
            pltpu.make_async_copy(piece.at[:, 0:128], q_scr.at[pl.ds(at, n)], sem.at[10 + len(qc)])
        )
        at += n
    for copy in kc + vc + qc:
        copy.start()
    v_scr[:, :, HD:, :] = jnp.ones((65, 2, 16, 128), BF)
    v_scr[64] = jnp.zeros((2, 80, 128), BF)
    low = lax.broadcasted_iota(jnp.int32, (128, 128), 1) < HD
    zero = jnp.zeros((128, 128), BF)
    for copy in kc:
        copy.wait()

    def split(i, carry):
        pair = kpk[i].reshape(128, 128)
        k_scr[2 * i] = jnp.where(low, pair, zero)
        k_scr[2 * i + 1] = jnp.where(low, zero, pair)
        return carry

    lax.fori_loop(0, 64, split, 0, unroll=4)
    for copy in vc + qc:
        copy.wait()
    per = nq // streams

    def total(s):
        return lax.fori_loop(s * per, (s + 1) * per, lambda q, t: t + cnt[q], jnp.int32(0))

    steps = total(0)
    for s in range(1, streams):
        steps = jnp.maximum(steps, total(s))

    def row(s, q):
        return jnp.minimum(q, (s + 1) * per - 1)

    def first(s, q, j):
        qr = row(s, q)
        base = qr * NBR + 2 * j
        qt = q_scr[lax.shift_right_logical(qr, 1), pl.ds(pl.multiple_of((qr & 1) * HD, HD), HD), :]
        keys = jnp.concatenate([k_scr[kidx[base]], k_scr[kidx[base + 1]]], axis=0)
        scores = jnp.dot(keys, jnp.concatenate([qt, qt], axis=0), preferred_element_type=F32)
        s_bufs[s][...] = scores
        return jnp.max(scores.reshape(32, 8, 128), axis=0)

    def second(s, q, j, top, m, acc):
        qr = row(s, q)
        base = qr * NBR + 2 * j
        va, vb = vidx[base], vidx[base + 1]
        m = jnp.where(j == 0, LOW, m)
        m_new = jnp.maximum(m, jnp.max(top, axis=0, keepdims=True))
        mc = m_new * SCALE2
        powers = jnp.exp2(s_bufs[s][...] * SCALE2 - mc).astype(BF)
        values = jnp.concatenate(
            [v_scr[lax.shift_right_logical(va, 1), va & 1], v_scr[lax.shift_right_logical(vb, 1), vb & 1]],
            axis=1,
        )
        acc = acc * jnp.exp2(m * SCALE2 - mc) + jnp.dot(values, powers, preferred_element_type=F32)
        l = acc[HD : HD + 1]
        lc = jnp.maximum(l, 1.0)
        to = jnp.where(q >= (s + 1) * per, nq, qr)
        o_scr[to] = (acc[:HD] * (1.0 / lc)).astype(BF)
        l_scr[pl.ds(to, 1), :] = jnp.where(l > 0, mc + jnp.log2(lc), LOW)
        last = j + 1 >= cnt[qr]
        return jnp.where(last, q + 1, q), jnp.where(last, 0, j + 1), m_new, acc

    def body(t, carry):
        state, tops = list(carry[0]), list(carry[1])
        for s in range(streams):
            after = (s + ahead) % streams
            tops.append(first(after, state[after][0], state[after][1]))
            q, j, m, acc = state[s]
            state[s] = second(s, q, j, tops.pop(0), m, acc)
        return tuple(state), tuple(tops)

    start = tuple(
        (jnp.int32(s * per), jnp.int32(0), jnp.full((1, 128), LOW, F32), jnp.zeros((80, 128), F32))
        for s in range(streams)
    )
    tops = tuple(first(s, jnp.int32(s * per), jnp.int32(0)) for s in range(ahead))
    lax.fori_loop(0, steps, body, (start, tops))
    copies = []
    for s in range(len(slots)):
        lse = l_scr[32 * s : 32 * (s + 1)]
        high = lse.astype(BF)
        rest = lse - high.astype(F32)
        mid = rest.astype(BF)
        tail = (rest - mid.astype(F32)).astype(BF)
        extra = o_scr.at[nq + 1 + 2 * s]
        extra[0:32] = high
        extra[32:64] = mid
        o_scr[nq + 2 + 2 * s] = jnp.concatenate([tail, tail], axis=0)
        copies.append(
            pltpu.make_async_copy(o_scr.at[pl.ds(32 * s, 32)], outs[s].at[pl.ds(0, 32)], osem.at[2 * s])
        )
        copies.append(
            pltpu.make_async_copy(
                o_scr.at[pl.ds(nq + 1 + 2 * s, 2)], outs[s].at[pl.ds(32, 2)], osem.at[2 * s + 1]
            )
        )
    for copy in copies:
        copy.start()
    for copy in copies:
        copy.wait()


def attend(lists, at, rows, kvs, streams, ahead):
    slots = [[p.shape[0] for p in s] for s in rows]
    flat = [p for s in rows for p in s]
    nq = 32 * len(slots)
    kidx, vidx, cnt = (v[at : at + nq].reshape(-1) for v in lists)
    anywhere = pl.BlockSpec(memory_space=pl.ANY)
    return pl.pallas_call(
        functools.partial(attend_kernel, streams, ahead, slots),
        out_shape=[jax.ShapeDtypeStruct((34, HD, 128), BF)] * len(slots),
        in_specs=[pl.BlockSpec(memory_space=pltpu.SMEM)] * 3 + [anywhere] * (len(flat) + 5),
        out_specs=[anywhere] * len(slots),
        scratch_shapes=[
            pltpu.VMEM((64, 2, 64, 128), BF),
            pltpu.VMEM((128, 128, 128), BF),
            pltpu.VMEM((65, 2, 80, 128), BF),
            pltpu.VMEM((nq // 2, 128, 128), BF),
            pltpu.VMEM((nq + 1 + 2 * len(slots), HD, 128), BF),
            pltpu.VMEM((nq + 8, 128), F32),
            pltpu.SemaphoreType.DMA((16,)),
            pltpu.SemaphoreType.DMA((8,)),
        ]
        + [pltpu.VMEM((256, 128), F32)] * streams,
        cost_estimate=pl.CostEstimate(
            flops=nq * 8 * 128 * 128 * 256, bytes_accessed=8 << 20, transcendentals=nq * 8 * 128 * 128
        ),
        name="attend",
    )(kidx, vidx, cnt, *flat, *kvs)


def merge_kernel(a_ref, b_ref, c_ref, d_ref, o_ref):
    refs = (a_ref, b_ref, c_ref, d_ref)
    lses = [
        r[32, 0:32].astype(F32) + r[32, 32:64].astype(F32) + r[33, 0:32].astype(F32) for r in refs
    ]
    top = functools.reduce(jnp.maximum, lses)
    weights = [jnp.exp2(l - top) for l in lses]
    scale = 1.0 / sum(weights)
    weights = [w * scale for w in weights]
    for q in range(32):
        o_ref[q] = sum(r[q].astype(F32) * w[q : q + 1] for r, w in zip(refs, weights)).astype(BF)


def merge(parts):
    return pl.pallas_call(
        merge_kernel,
        out_shape=jax.ShapeDtypeStruct((32, HD, 128), BF),
        name="merge",
    )(*parts)


def index_lists(slabs):
    v = slabs.astype(F32).reshape(64, 2, 2, NBR)
    ids = (v[:, :, 0] * 16 + v[:, :, 1]).astype(jnp.int32).reshape(128, NBR)
    core = lax.axis_index("c")
    xb, yb = ids // 128, ids // 8 % 4
    xm, ym = lax.axis_index("x"), lax.axis_index("y")
    valid = jnp.where(core == 0, xb == xm, yb == ym)
    ring = jnp.where(core == 0, yb - ym, xb - xm) & 3
    slot = jnp.where(ring == 0, 0, jnp.where(ring == 3, 1, ring + 1))
    local = slot * 32 + (ids // 32 % 4) * 8 + ids % 8
    before = jnp.arange(NBR)[:, None] < jnp.arange(NBR)[None, :]
    place = jnp.sum(jnp.where(before[None] & valid[:, :, None], 1, 0), axis=1)
    hit = valid[:, None, :] & (place[:, None, :] == jnp.arange(NBR)[None, :, None])
    found = jnp.sum(jnp.where(hit, local[:, None, :] + 1, 0), axis=2) - 1
    count = jnp.sum(valid.astype(jnp.int32), axis=1)
    vidx = jnp.where(found < 0, NULL, found)
    kidx = jnp.where(found < 0, jnp.maximum(found[:, :1], 0), found)
    return kidx, vidx, jnp.maximum((count + 1) // 2, 1)


def shards(qkv_rows, neighbours, w_out):
    mine = lax.axis_index("y") * 4 + lax.axis_index("zl") * 2 + lax.axis_index("c")
    own = lax.dynamic_slice(neighbours, (2 * mine, 0), (2, NBR))
    digits = jnp.stack([own // 16, own % 16], axis=1).reshape(1, 128).astype(BF)
    slab = jnp.broadcast_to(digits, (16, 128))
    chunks = lax.all_to_all(pack(qkv_rows, slab), ZC, split_axis=0, concat_axis=0, tiled=True)
    kv, rows = chunks[:, :256], chunks[:, 256:]
    kv_l, kv_r = move_keys(kv, 1), move_keys(kv, -1)
    q_l, q_r = move_rows(rows, 1), move_rows(rows, -1)
    kv_d0, kv_d1 = move_keys(kv_l[:8], 1), move_keys(kv_r[8:], -1)
    q_d0, q_d1 = move_rows(q_l[:8], 1), move_rows(q_r[8:], -1)
    lists = index_lists(jnp.concatenate([v[:, 128] for v in (rows, q_l, q_r, q_d0, q_d1)], axis=0))
    kvs = [v.reshape(-1, 4, 64, 128) for v in (kv, kv_l, kv_r, kv_d0, kv_d1)]
    far = attend(lists, 32, [[q_l], [q_r], [q_d0, q_d1]], kvs, 8, 6)
    near = attend(lists, 0, [[rows]], kvs, 8, 6)
    back = [move_rows(v, step) for v, step in zip(far, (-1, 1, 2))]
    attended = merge([near[0], *back]).reshape(16, 128, 128)
    arrived = lax.all_to_all(attended, ZC, split_axis=0, concat_axis=0, tiled=True)
    out = jnp.einsum(
        "hbdt,hdo->bto",
        arrived.reshape(16, 2, HD, 128),
        w_out.reshape(16, HD, 1024),
        preferred_element_type=F32,
    )
    return out.astype(BF).reshape(256, 1024)


def solution(mesh):
    grid = Mesh(mesh.devices.reshape(4, 4, 4, 2, 2), AXES)
    return jax.shard_map(
        shards,
        mesh=grid,
        in_specs=(P(AXES, None, None), P(("x", "zh"), None), P()),
        out_specs=P(AXES, None),
        check_vma=False,
    )
```
